32 devices in a mesh: pipe: 4 (over x, core), dp: 2 (over y), tensor: 4 (over z).
Axes of the slice: x: 2, y: 2, z: 4, core: 2. Of those that a mesh axis runs over, the one named last changes fastest.
Arguments:
- grad_top: bfloat16 [2, 128, 12288], P(None, None, ('dp', 'tensor')), may hold values from -1.1953125 to 1.1953125
- inputs: bfloat16 [4, 2, 128, 12288], P('pipe', None, None, ('dp', 'tensor')), may hold values from -6 to 6
- pre: bfloat16 [4, 2, 128, 6144], P('pipe', None, 'dp', 'tensor'), may hold values from -6 to 6
- weight_in: bfloat16 [4, 6144, 12288], P('pipe', 'tensor', 'dp'), may hold values from -0.0546875 to 0.0546875
- weight_out: bfloat16 [4, 6144, 12288], P('pipe', 'tensor', 'dp'), may hold values from -0.0546875 to 0.0546875
Outputs:
- weight_in_grad: bfloat16 [4, 6144, 12288], P('pipe', 'tensor', 'dp')
- weight_out_grad: bfloat16 [4, 6144, 12288], P('pipe', 'tensor', 'dp')
- section_grads: bfloat16 [4, 2, 128, 12288], P('pipe', None, None, ('dp', 'tensor'))
The draws below stay inside these ranges and needn't reach their ends.
All inputs are finite; a program needn't handle non-finite values.
Results may differ from the reference program's by a relative error of at most 0.024.
Values may be sent and summed in bfloat16 or wider, within the bound.
A program may use at most 512 MiB of HBM per device.

```python
import math
import jax
import jax.numpy as jnp
from jax import lax

D = 12288
ROWS = 128
MB = 2
HD = 6144
N_PIPE = 4
N_TENSOR = 4


def steps_of(own_key, shape, split, low, high):
    level = 1.0
    for dim, parts in split:
        heights = jax.random.uniform(jax.random.fold_in(jax.random.fold_in(own_key, 6), dim), (parts,), jnp.float32, low / len(split), high / len(split))
        level = level * jnp.repeat(jnp.exp(heights), shape[dim] // parts).reshape((-1,) + (1,) * (len(shape) - 1 - dim))
    return level


def bell_draw(rng, shape, width, limit, shards=(), held_as=jnp.bfloat16):
    array = width * jax.random.normal(rng, shape, jnp.float32)
    if shards:
        array = array * steps_of(rng, shape, shards, -0.22, 0.18)
    return jnp.clip(array, -limit, limit).astype(held_as)


def setup_inputs(seed: int = 0) -> dict:
    keys = jax.random.split(jax.random.key(seed), 6)
    grad_top = bell_draw(keys[0], (MB, ROWS, D), 0.2, 1.1953125, ((2, 8),))
    inputs = bell_draw(keys[1], (N_PIPE, MB, ROWS, D), 1.0, 6.0, ((0, 4), (3, 8)))
    pre = bell_draw(keys[2], (N_PIPE, MB, ROWS, HD), 1.0, 6.0, ((0, 4), (2, 2), (3, 4)))
    weight_in = bell_draw(keys[3], (N_PIPE, HD, D), D ** -0.5, 0.0546875, ((0, 4), (1, 4), (2, 2)))
    weight_out = bell_draw(keys[4], (N_PIPE, HD, D), D ** -0.5, 0.0546875, ((0, 4), (1, 4), (2, 2)))
    return dict(grad_top=grad_top, inputs=inputs, pre=pre, weight_in=weight_in, weight_out=weight_out)


def gelu_pair(values):
    root_coef = math.sqrt(2.0 / math.pi)
    inner = root_coef * (values + 0.044715 * values * values * values)
    tangent = jnp.tanh(inner)
    activ = 0.5 * values * (1.0 + tangent)
    slope = 0.5 * (1.0 + tangent) + 0.5 * values * (1.0 - tangent * tangent) * root_coef * (1.0 + 3.0 * 0.044715 * values * values)
    return (activ, slope)

def reference(grad_top, inputs, pre, weight_in, weight_out):
    current = grad_top
    grads_list = []
    in_list = []
    out_list = []
    group_width = HD // N_TENSOR
    for section_index in range(N_PIPE - 1, -1, -1):
        layer_in = weight_in[section_index]
        layer_out = weight_out[section_index]
        flat_grad = current.reshape(-1, D)
        flat_input = inputs[section_index].reshape(-1, D)
        flat_pre = pre[section_index].reshape(-1, HD).astype(jnp.float32)
        head_grad = jnp.dot(flat_grad, layer_out.T, preferred_element_type=jnp.float32)
        activ, slope = gelu_pair(flat_pre)
        head_delta = (head_grad * slope).astype(jnp.bfloat16)
        activated = activ.astype(jnp.bfloat16)
        blocks = head_delta.reshape(-1, N_TENSOR, group_width)
        weight_blocks = layer_in.reshape(N_TENSOR, group_width, D)

        def add_block(total, block_index):
            left = lax.dynamic_index_in_dim(blocks, block_index, 1, False)
            right = lax.dynamic_index_in_dim(weight_blocks, block_index, 0, False)
            piece = jnp.dot(left, right, preferred_element_type=jnp.float32)
            rounded = lax.optimization_barrier(piece.astype(jnp.bfloat16))
            return (total + rounded.astype(jnp.float32), None)
        summed, unused = lax.scan(add_block, jnp.zeros(flat_grad.shape, jnp.float32), jnp.arange(N_TENSOR, dtype=jnp.int32))
        new_grad = (flat_grad.astype(jnp.float32) + summed).astype(jnp.bfloat16)
        grad_out_w = jnp.dot(activated.T, flat_grad, preferred_element_type=jnp.float32)
        grad_in_w = jnp.dot(head_delta.T, flat_input, preferred_element_type=jnp.float32)
        grads_list.insert(0, new_grad.reshape(current.shape))
        in_list.insert(0, grad_in_w.astype(jnp.bfloat16))
        out_list.insert(0, grad_out_w.astype(jnp.bfloat16))
        current = new_grad.reshape(current.shape)
    return (jnp.stack(in_list), jnp.stack(out_list), jnp.stack(grads_list))
```

```python
import functools
import math

import jax
import jax.numpy as jnp
from jax import lax
from jax.experimental import pallas as pl
from jax.experimental.pallas import tpu as pltpu
from jax.sharding import PartitionSpec as P


def shifted(block, axis, distance):
    devices = range(lax.axis_size(axis))
    route = [(i - distance, i) for i in devices if i - distance in devices]
    return lax.ppermute(block, axis, route)


def gelu_pair(values):
    root_coef = math.sqrt(2.0 / math.pi)
    inner = root_coef * (values + 0.044715 * values * values * values)
    tangent = jnp.tanh(inner)
    activ = 0.5 * values * (1.0 + tangent)
    slope = 0.5 * (1.0 + tangent) + 0.5 * values * (1.0 - tangent * tangent) * root_coef * (
        1.0 + 3.0 * 0.044715 * values * values
    )
    return (activ, slope)


def general_device(grad_top, inputs, pre, weight_in, weight_out):
    sections = lax.axis_size("pipe")
    section = lax.axis_index("pipe")
    micro = grad_top.shape[0]
    local_in = weight_in[0]
    local_out = weight_out[0]
    contract = (((0,), (0,)), ((), ()))
    accum_in = jnp.zeros(local_in.shape, jnp.float32)
    accum_out = jnp.zeros(local_out.shape, jnp.float32)
    grads_out = jnp.zeros(grad_top.shape, jnp.bfloat16)
    outgoing = grad_top[0]
    for timestep in range(micro + sections - 1):
        micro_index = timestep - (sections - 1 - section)
        valid = jnp.logical_and(micro_index >= 0, micro_index < micro)
        clipped = jnp.clip(micro_index, 0, micro - 1)
        top_grad = lax.dynamic_index_in_dim(grad_top, clipped, 0, False)
        if timestep == 0:
            current = top_grad
        else:
            received = shifted(outgoing, "pipe", -1)
            current = jnp.where(section == sections - 1, top_grad, received)
        layer_input = lax.dynamic_index_in_dim(inputs[0], clipped, 0, False)
        pre_local = lax.dynamic_index_in_dim(pre[0], clipped, 0, False)
        grad_cols, input_cols = (
            lax.all_gather(current, "tensor", axis=1, tiled=True),
            lax.all_gather(layer_input, "tensor", axis=1, tiled=True),
        )
        head_part = lax.dot_general(
            grad_cols, local_out, (((1,), (1,)), ((), ())), preferred_element_type=jnp.float32
        )
        head_grad = lax.psum(head_part.astype(jnp.bfloat16), "dp").astype(jnp.float32)
        pre_all = lax.all_gather(pre_local, "dp", axis=0, tiled=True)
        activ, slope = gelu_pair(pre_all.astype(jnp.float32))
        head_delta = (head_grad * slope).astype(jnp.bfloat16)
        activated = activ.astype(jnp.bfloat16)
        partial_value = jnp.dot(head_delta, local_in, preferred_element_type=jnp.float32)
        summed = lax.psum_scatter(
            partial_value.astype(jnp.bfloat16), "tensor", scatter_dimension=1, tiled=True
        ).astype(jnp.float32)
        new_grad = (current.astype(jnp.float32) + summed).astype(jnp.bfloat16)
        out_term = lax.dot_general(
            activated, grad_cols, contract, preferred_element_type=jnp.float32
        )
        in_term = lax.dot_general(
            head_delta, input_cols, contract, preferred_element_type=jnp.float32
        )
        accum_out = accum_out + jnp.where(valid, out_term, 0.0)
        accum_in = accum_in + jnp.where(valid, in_term, 0.0)
        previous = lax.dynamic_index_in_dim(grads_out, clipped, 0, False)
        grads_out = lax.dynamic_update_index_in_dim(
            grads_out, jnp.where(valid, new_grad, previous), clipped, 0
        )
        outgoing = new_grad
    return (
        accum_in.astype(jnp.bfloat16)[None],
        accum_out.astype(jnp.bfloat16)[None],
        grads_out[None],
    )


MESH = pl.DeviceIdType.MESH
CHUNK = 64
HEAD_TILE = 256
COL_TILE = 512
VMEM_BYTES = 62 * 2**20


def chain_kernel(
    dims,
    gtop, pre, inputs, win, wout,
    gall_o, xall_o, hd_o, act_o, sg_o,
    wi, wo, gbuf, rs_out, rs_in, dp_out, dp_in, slope, hg, pre_s, act, hd, newg, xs,
    w_sem, top_send, top_own, g_send, g_recv, rs_send, rs_recv, dp_send, dp_recv,
    pre_send, pre_recv, pre_own, x_send, x_recv, x_own, out_sem,
):
    sections, dps, tensors, chunks, chunk_rows, micro, block_rows = dims
    s = lax.axis_index("pipe")
    d = lax.axis_index("dp")
    t = lax.axis_index("tensor")
    heads, wide = wo.shape
    cols = wide // tensors
    is_top = s == sections - 1
    has_next = s > 0

    def wrap(value, size):
        return lax.rem(value + size, size)

    def column(index):
        return pl.ds(pl.multiple_of(index * cols, 128), cols)

    def row(c):
        return pl.ds(pl.multiple_of(c * chunk_rows, chunk_rows), chunk_rows)

    def remote(src, dst, send, recv, device):
        return pltpu.make_async_remote_copy(
            src_ref=src, dst_ref=dst, send_sem=send, recv_sem=recv,
            device_id=device, device_id_type=MESH,
        )

    copy_wo = pltpu.make_async_copy(wout, wo, w_sem.at[0])
    copy_wi = pltpu.make_async_copy(win, wi, w_sem.at[1])

    barrier = pltpu.get_barrier_semaphore()
    for k in range(1, tensors):
        pl.semaphore_signal(
            barrier, inc=1, device_id=(s, d, wrap(t + k, tensors)), device_id_type=MESH)
    for k in range(1, dps):
        pl.semaphore_signal(
            barrier, inc=1, device_id=(s, wrap(d + k, dps), t), device_id_type=MESH)

    for hop in (1, sections - 1):
        for k in range(tensors):
            pl.semaphore_signal(
                barrier, inc=1, device_id=(wrap(s + hop, sections), d, k), device_id_type=MESH)
    pl.semaphore_wait(barrier, (tensors - 1) + (dps - 1) + 2 * tensors)

    def top_copy(c, k):
        return remote(
            gtop.at[row(c), :], gbuf.at[row(c), column(t)],
            top_send.at[c, k - 1], g_recv.at[c, t], (s, d, wrap(t + k, tensors)))

    def top_local(c):
        return pltpu.make_async_copy(
            gtop.at[row(c), :], gbuf.at[row(c), column(t)], top_own.at[c])

    def relay_copy(c, k):
        return remote(
            newg.at[row(c), :], gbuf.at[row(c), column(t)],
            g_send.at[c, k], g_recv.at[c, t], (s - 1, d, k))

    def arrival(c, source):
        return remote(
            newg.at[row(c), :], gbuf.at[row(c), column(source)],
            g_send.at[c, 0], g_recv.at[c, source], (s, d, t))

    def pre_copy(m, k):
        return remote(
            pre.at[m], pre_s.at[pl.ds(pl.multiple_of((m * dps + d) * block_rows, 16), block_rows), :],
            pre_send.at[m, k - 1], pre_recv.at[m, k - 1], (s, wrap(d + k, dps), t))

    def pre_arrival(m, k):
        source = wrap(d - k, dps)
        return remote(
            pre.at[m], pre_s.at[pl.ds(pl.multiple_of((m * dps + source) * block_rows, 16), block_rows), :],
            pre_send.at[m, k - 1], pre_recv.at[m, k - 1], (s, wrap(d + k, dps), t))

    def pre_local(m):
        return pltpu.make_async_copy(
            pre.at[m], pre_s.at[pl.ds(pl.multiple_of((m * dps + d) * block_rows, 16), block_rows), :],
            pre_own.at[m])

    def x_copy(k):
        return remote(
            inputs, xall_o.at[:, column(t)],
            x_send.at[k - 1], x_recv.at[k - 1], (s, d, wrap(t + k, tensors)))

    def x_arrival(k):
        return remote(
            inputs, xall_o.at[:, column(wrap(t - k, tensors))],
            x_send.at[k - 1], x_recv.at[k - 1], (s, d, wrap(t + k, tensors)))

    def dp_copy(c, k):
        return remote(
            dp_out.at[row(c), :], dp_in.at[k - 1, row(c), :],
            dp_send.at[c, k - 1], dp_recv.at[c, k - 1], (s, wrap(d + k, dps), t))

    def rs_copy(c, k):
        target = wrap(t + k, tensors)
        return remote(
            rs_out.at[row(c), column(target)], rs_in.at[k - 1, row(c), :],
            rs_send.at[c, k - 1], rs_recv.at[c, k - 1], (s, d, target))

    for m in range(micro):
        for k in range(1, dps):
            pre_copy(m, k).start()
        pre_local(m).start()

    @pl.when(is_top)
    def _():
        @pl.loop(0, chunks)
        def _(c):
            top_local(c).start()
            for k in range(1, tensors):
                top_copy(c, k).start()

    copy_wo.start()
    copy_wi.start()
    early = 2 * s < sections

    @pl.when(early)
    def _():
        for k in range(1, tensors):
            x_copy(k).start()

    x_in = pltpu.make_async_copy(inputs, xs, x_own.at[0])
    x_out = pltpu.make_async_copy(xs, xall_o.at[:, column(t)], x_own.at[1])
    x_in.start()

    for m in range(micro):
        pre_local(m).wait()
        for k in range(1, dps):
            pre_arrival(m, k).wait_recv()

    @pl.loop(0, pre_s.shape[0] // 16)
    def _(b):
        rows = pl.ds(pl.multiple_of(b * 16, 16), 16)
        activ, steep = gelu_pair(pre_s[rows, :].astype(jnp.float32))
        act[rows, :] = activ.astype(jnp.bfloat16)
        slope[rows, :] = steep

    x_in.wait()
    x_out.start()
    act_out = pltpu.make_async_copy(act, act_o, out_sem.at[0])
    act_out.start()
    copy_wo.wait()

    def chunk_step(c):
        @pl.when(is_top)
        def _():
            top_local(c).wait()
            for k in range(1, tensors):
                arrival(c, wrap(t + k, tensors)).wait_recv()

        @pl.when(jnp.logical_not(is_top))
        def _():
            for k in range(tensors):
                arrival(c, k).wait_recv()

        @pl.loop(0, heads // HEAD_TILE)
        def _(j):
            tile = pl.ds(pl.multiple_of(j * HEAD_TILE, HEAD_TILE), HEAD_TILE)
            part = lax.dot_general(
                gbuf[row(c), :], wo[tile, :], (((1,), (1,)), ((), ())),
                preferred_element_type=jnp.float32)
            hg[:, tile] = part
            dp_out[row(c), tile] = part.astype(jnp.bfloat16)

        for k in range(1, dps):
            dp_copy(c, k).start()

        @pl.when(c == 0)
        def _():
            copy_wi.wait()

        for k in range(1, dps):
            dp_copy(c, k).wait_recv()
        total = hg[...]
        for k in range(1, dps):
            total = total + dp_in[k - 1, row(c), :].astype(jnp.float32)
        hd[row(c), :] = (total * slope[row(c), :]).astype(jnp.bfloat16)

        for k in list(range(1, tensors)) + [0]:
            base = wrap(t + k, tensors) * cols

            @pl.loop(0, cols // COL_TILE)
            def _(j):
                tile = pl.ds(pl.multiple_of(base + j * COL_TILE, 128), COL_TILE)
                rs_out[row(c), tile] = jnp.dot(
                    hd[row(c), :], wi[:, tile], preferred_element_type=jnp.float32
                ).astype(jnp.bfloat16)

            if k:
                rs_copy(c, k).start()

        for k in range(1, tensors):
            rs_copy(c, k).wait_recv()
        summed = rs_out[row(c), column(t)].astype(jnp.float32)
        for k in range(1, tensors):
            summed = summed + rs_in[k - 1, row(c), :].astype(jnp.float32)
        newg[row(c), :] = (
            gbuf[row(c), column(t)].astype(jnp.float32) + summed).astype(jnp.bfloat16)

        @pl.when(has_next)
        def _():
            for k in range(tensors):
                relay_copy(c, k).start()

    @pl.loop(0, chunks)
    def _(c):
        chunk_step(c)

    @pl.when(jnp.logical_not(early))
    def _():
        for k in range(1, tensors):
            x_copy(k).start()

    outs = [
        pltpu.make_async_copy(gbuf, gall_o, out_sem.at[1]),
        pltpu.make_async_copy(hd, hd_o, out_sem.at[2]),
        pltpu.make_async_copy(newg, sg_o, out_sem.at[3]),
    ]
    for copy in outs:
        copy.start()

    for m in range(micro):
        for k in range(1, dps):
            pre_copy(m, k).wait_send()

    @pl.loop(0, chunks)
    def _(c):
        for k in range(1, dps):
            dp_copy(c, k).wait_send()
        for k in range(1, tensors):
            rs_copy(c, k).wait_send()

        @pl.when(is_top)
        def _():
            for k in range(1, tensors):
                top_copy(c, k).wait_send()

        @pl.when(has_next)
        def _():
            for k in range(tensors):
                relay_copy(c, k).wait_send()

    x_out.wait()
    act_out.wait()
    for copy in outs:
        copy.wait()
    for k in range(1, tensors):
        x_copy(k).wait_send()
        x_arrival(k).wait_recv()


def chain(sizes, gtop, pre, inputs, win, wout):
    sections, dps, tensors = sizes
    rows, cols = gtop.shape
    micro, block_rows, heads = pre.shape
    wide = wout.shape[1]
    chunks = rows // CHUNK
    dims = (sections, dps, tensors, chunks, CHUNK, micro, block_rows)
    bf16, f32 = jnp.bfloat16, jnp.float32
    anywhere = pl.BlockSpec(memory_space=pl.ANY)
    dma = pltpu.SemaphoreType.DMA
    return pl.pallas_call(
        functools.partial(chain_kernel, dims),
        out_shape=(
            jax.ShapeDtypeStruct((rows, wide), bf16),
            jax.ShapeDtypeStruct((rows, wide), bf16),
            jax.ShapeDtypeStruct((rows, heads), bf16),
            jax.ShapeDtypeStruct((rows, heads), bf16),
            jax.ShapeDtypeStruct((rows, cols), bf16),
        ),
        in_specs=[anywhere] * 5,
        out_specs=(anywhere,) * 5,
        scratch_shapes=[
            pltpu.VMEM((heads, wide), bf16),
            pltpu.VMEM((heads, wide), bf16),
            pltpu.VMEM((rows, wide), bf16),
            pltpu.VMEM((rows, wide), bf16),
            pltpu.VMEM((tensors - 1, rows, cols), bf16),
            pltpu.VMEM((rows, heads), bf16),
            pltpu.VMEM((dps - 1, rows, heads), bf16),
            pltpu.VMEM((rows, heads), f32),
            pltpu.VMEM((CHUNK, heads), f32),
            pltpu.VMEM((rows, heads), bf16),
            pltpu.VMEM((rows, heads), bf16),
            pltpu.VMEM((rows, heads), bf16),
            pltpu.VMEM((rows, cols), bf16),
            pltpu.VMEM((rows, cols), bf16),
            dma((2,)),
            dma((chunks, tensors - 1)),
            dma((chunks,)),
            dma((chunks, tensors)),
            dma((chunks, tensors)),
            dma((chunks, tensors - 1)),
            dma((chunks, tensors - 1)),
            dma((chunks, dps - 1)),
            dma((chunks, dps - 1)),
            dma((micro, dps - 1)),
            dma((micro, dps - 1)),
            dma((micro,)),
            dma((tensors - 1,)),
            dma((tensors - 1,)),
            dma((2,)),
            dma((4,)),
        ],
        compiler_params=pltpu.CompilerParams(
            collective_id=0, has_side_effects=True, vmem_limit_bytes=VMEM_BYTES),
        name="chain",
    )(gtop, pre, inputs, win, wout)


def kernel_fits(sizes, grad_top, pre, weight_out):
    sections, dps, tensors = sizes
    micro, tokens, cols = grad_top.shape
    heads, wide = weight_out.shape[1:]
    rows = micro * tokens
    need = 4 * heads * wide + 2 * rows * (3 * wide + (7 + dps) * heads + 2 * cols)
    return (
        dps > 1 and tensors > 1 and sections > 1
        and cols % COL_TILE == 0 and heads % HEAD_TILE == 0
        and rows % CHUNK == 0 and pre.shape[2] % 16 == 0
        and need + 4 * CHUNK * heads < VMEM_BYTES - 2**21
    )


def on_device(grad_top, inputs, pre, weight_in, weight_out):
    sizes = tuple(lax.axis_size(name) for name in ("pipe", "dp", "tensor"))
    if not kernel_fits(sizes, grad_top, pre, weight_out):
        return general_device(grad_top, inputs, pre, weight_in, weight_out)
    cols = grad_top.shape[-1]
    gall, xall, head_delta, activated, new_grad = chain(
        sizes,
        grad_top.reshape(-1, cols),
        pre[0],
        inputs[0].reshape(-1, cols),
        weight_in[0],
        weight_out[0],
    )
    contract = (((0,), (0,)), ((), ()))
    grad_out = lax.dot_general(activated, gall, contract, preferred_element_type=jnp.float32)
    grad_in = lax.dot_general(head_delta, xall, contract, preferred_element_type=jnp.float32)
    return (
        grad_in.astype(jnp.bfloat16)[None],
        grad_out.astype(jnp.bfloat16)[None],
        new_grad.reshape(grad_top.shape)[None],
    )


def solution(mesh):
    placed = (
        P(None, None, ("dp", "tensor")),
        P("pipe", None, None, ("dp", "tensor")),
        P("pipe", None, "dp", "tensor"),
        P("pipe", "tensor", "dp"),
        P("pipe", "tensor", "dp"),
    )
    return jax.shard_map(
        on_device,
        mesh=mesh,
        in_specs=placed,
        out_specs=(
            P("pipe", "tensor", "dp"),
            P("pipe", "tensor", "dp"),
            P("pipe", None, None, ("dp", "tensor")),
        ),
        check_vma=False,
    )
```

```python
import functools
import math

import jax
import jax.numpy as jnp
from jax import lax
from jax.experimental import pallas as pl
from jax.experimental.pallas import tpu as pltpu
from jax.sharding import PartitionSpec as P


def shifted(block, axis, distance):
    devices = range(lax.axis_size(axis))
    route = [(i - distance, i) for i in devices if i - distance in devices]
    return lax.ppermute(block, axis, route)


def gelu_pair(values):
    root_coef = math.sqrt(2.0 / math.pi)
    inner = root_coef * (values + 0.044715 * values * values * values)
    tangent = jnp.tanh(inner)
    activ = 0.5 * values * (1.0 + tangent)
    slope = 0.5 * (1.0 + tangent) + 0.5 * values * (1.0 - tangent * tangent) * root_coef * (
        1.0 + 3.0 * 0.044715 * values * values
    )
    return (activ, slope)


def general_device(grad_top, inputs, pre, weight_in, weight_out):
    sections = lax.axis_size("pipe")
    section = lax.axis_index("pipe")
    micro = grad_top.shape[0]
    local_in = weight_in[0]
    local_out = weight_out[0]
    contract = (((0,), (0,)), ((), ()))
    accum_in = jnp.zeros(local_in.shape, jnp.float32)
    accum_out = jnp.zeros(local_out.shape, jnp.float32)
    grads_out = jnp.zeros(grad_top.shape, jnp.bfloat16)
    outgoing = grad_top[0]
    for timestep in range(micro + sections - 1):
        micro_index = timestep - (sections - 1 - section)
        valid = jnp.logical_and(micro_index >= 0, micro_index < micro)
        clipped = jnp.clip(micro_index, 0, micro - 1)
        top_grad = lax.dynamic_index_in_dim(grad_top, clipped, 0, False)
        if timestep == 0:
            current = top_grad
        else:
            received = shifted(outgoing, "pipe", -1)
            current = jnp.where(section == sections - 1, top_grad, received)
        layer_input = lax.dynamic_index_in_dim(inputs[0], clipped, 0, False)
        pre_local = lax.dynamic_index_in_dim(pre[0], clipped, 0, False)
        grad_cols, input_cols = (
            lax.all_gather(current, "tensor", axis=1, tiled=True),
            lax.all_gather(layer_input, "tensor", axis=1, tiled=True),
        )
        head_part = lax.dot_general(
            grad_cols, local_out, (((1,), (1,)), ((), ())), preferred_element_type=jnp.float32
        )
        head_grad = lax.psum(head_part.astype(jnp.bfloat16), "dp").astype(jnp.float32)
        pre_all = lax.all_gather(pre_local, "dp", axis=0, tiled=True)
        activ, slope = gelu_pair(pre_all.astype(jnp.float32))
        head_delta = (head_grad * slope).astype(jnp.bfloat16)
        activated = activ.astype(jnp.bfloat16)
        partial_value = jnp.dot(head_delta, local_in, preferred_element_type=jnp.float32)
        summed = lax.psum_scatter(
            partial_value.astype(jnp.bfloat16), "tensor", scatter_dimension=1, tiled=True
        ).astype(jnp.float32)
        new_grad = (current.astype(jnp.float32) + summed).astype(jnp.bfloat16)
        out_term = lax.dot_general(
            activated, grad_cols, contract, preferred_element_type=jnp.float32
        )
        in_term = lax.dot_general(
            head_delta, input_cols, contract, preferred_element_type=jnp.float32
        )
        accum_out = accum_out + jnp.where(valid, out_term, 0.0)
        accum_in = accum_in + jnp.where(valid, in_term, 0.0)
        previous = lax.dynamic_index_in_dim(grads_out, clipped, 0, False)
        grads_out = lax.dynamic_update_index_in_dim(
            grads_out, jnp.where(valid, new_grad, previous), clipped, 0
        )
        outgoing = new_grad
    return (
        accum_in.astype(jnp.bfloat16)[None],
        accum_out.astype(jnp.bfloat16)[None],
        grads_out[None],
    )


MESH = pl.DeviceIdType.MESH
CHUNK = 64
HEAD_TILE = 512
COL_TILE = 512
VMEM_BYTES = 62 * 2**20


def chain_kernel(
    dims,
    gtop, pre, inputs, win, wout,
    gall_o, xall_o, hd_o, act_o, sg_o,
    wi, wo, gbuf, rs_out, rs_in, dp_out, dp_in, slope, hg, pre_s, act, hd, newg, xs,
    w_sem, top_send, top_own, g_send, g_recv, rs_send, rs_recv, dp_send, dp_recv,
    pre_send, pre_recv, pre_own, x_send, x_recv, x_own, out_sem,
):
    sections, dps, tensors, chunks, chunk_rows, micro, block_rows = dims
    s = lax.axis_index("pipe")
    d = lax.axis_index("dp")
    t = lax.axis_index("tensor")
    heads, wide = wo.shape
    cols = wide // tensors
    is_top = s == sections - 1
    has_next = s > 0

    def wrap(value, size):
        return lax.rem(value + size, size)

    def column(index):
        return pl.ds(pl.multiple_of(index * cols, 128), cols)

    def row(c):
        return pl.ds(pl.multiple_of(c * chunk_rows, chunk_rows), chunk_rows)

    def remote(src, dst, send, recv, device):
        return pltpu.make_async_remote_copy(
            src_ref=src, dst_ref=dst, send_sem=send, recv_sem=recv,
            device_id=device, device_id_type=MESH,
        )

    copy_wo = pltpu.make_async_copy(wout, wo, w_sem.at[0])
    copy_wi = pltpu.make_async_copy(win, wi, w_sem.at[1])

    barrier = pltpu.get_barrier_semaphore()
    for k in range(1, tensors):
        pl.semaphore_signal(
            barrier, inc=1, device_id=(s, d, wrap(t + k, tensors)), device_id_type=MESH)
    for k in range(1, dps):
        pl.semaphore_signal(
            barrier, inc=1, device_id=(s, wrap(d + k, dps), t), device_id_type=MESH)

    for hop in (1, sections - 1):
        for k in range(tensors):
            pl.semaphore_signal(
                barrier, inc=1, device_id=(wrap(s + hop, sections), d, k), device_id_type=MESH)
    pl.semaphore_wait(barrier, (tensors - 1) + (dps - 1) + 2 * tensors)

    def top_copy(c, k):
        return remote(
            gtop.at[row(c), :], gbuf.at[row(c), column(t)],
            top_send.at[c, k - 1], g_recv.at[c, t], (s, d, wrap(t + k, tensors)))

    def top_local(c):
        return pltpu.make_async_copy(
            gtop.at[row(c), :], gbuf.at[row(c), column(t)], top_own.at[c])

    def relay_copy(c, k):
        return remote(
            newg.at[row(c), :], gbuf.at[row(c), column(t)],
            g_send.at[c, k], g_recv.at[c, t], (s - 1, d, k))

    def arrival(c, source):
        return remote(
            newg.at[row(c), :], gbuf.at[row(c), column(source)],
            g_send.at[c, 0], g_recv.at[c, source], (s, d, t))

    def pre_copy(m, k):
        return remote(
            pre.at[m], pre_s.at[pl.ds(pl.multiple_of((m * dps + d) * block_rows, 16), block_rows), :],
            pre_send.at[m, k - 1], pre_recv.at[m, k - 1], (s, wrap(d + k, dps), t))

    def pre_arrival(m, k):
        source = wrap(d - k, dps)
        return remote(
            pre.at[m], pre_s.at[pl.ds(pl.multiple_of((m * dps + source) * block_rows, 16), block_rows), :],
            pre_send.at[m, k - 1], pre_recv.at[m, k - 1], (s, wrap(d + k, dps), t))

    def pre_local(m):
        return pltpu.make_async_copy(
            pre.at[m], pre_s.at[pl.ds(pl.multiple_of((m * dps + d) * block_rows, 16), block_rows), :],
            pre_own.at[m])

    def x_copy(k):
        return remote(
            inputs, xall_o.at[:, column(t)],
            x_send.at[k - 1], x_recv.at[k - 1], (s, d, wrap(t + k, tensors)))

    def x_arrival(k):
        return remote(
            inputs, xall_o.at[:, column(wrap(t - k, tensors))],
            x_send.at[k - 1], x_recv.at[k - 1], (s, d, wrap(t + k, tensors)))

    def dp_copy(c, k):
        return remote(
            dp_out.at[row(c), :], dp_in.at[k - 1, row(c), :],
            dp_send.at[c, k - 1], dp_recv.at[c, k - 1], (s, wrap(d + k, dps), t))

    def rs_copy(c, k):
        target = wrap(t + k, tensors)
        return remote(
            rs_out.at[row(c), column(target)], rs_in.at[k - 1, row(c), :],
            rs_send.at[c, k - 1], rs_recv.at[c, k - 1], (s, d, target))

    for m in range(micro):
        for k in range(1, dps):
            pre_copy(m, k).start()
        pre_local(m).start()

    @pl.when(is_top)
    def _():
        @pl.loop(0, chunks)
        def _(c):
            top_local(c).start()
            for k in range(1, tensors):
                top_copy(c, k).start()

    copy_wo.start()
    copy_wi.start()
    early = 2 * s < sections

    @pl.when(early)
    def _():
        for k in range(1, tensors):
            x_copy(k).start()

    x_in = pltpu.make_async_copy(inputs, xs, x_own.at[0])
    x_out = pltpu.make_async_copy(xs, xall_o.at[:, column(t)], x_own.at[1])
    x_in.start()

    for m in range(micro):
        pre_local(m).wait()
        for k in range(1, dps):
            pre_arrival(m, k).wait_recv()

    @pl.loop(0, pre_s.shape[0] // 16)
    def _(b):
        rows = pl.ds(pl.multiple_of(b * 16, 16), 16)
        activ, steep = gelu_pair(pre_s[rows, :].astype(jnp.float32))
        act[rows, :] = activ.astype(jnp.bfloat16)
        slope[rows, :] = steep

    x_in.wait()
    x_out.start()
    act_out = pltpu.make_async_copy(act, act_o, out_sem.at[0])
    act_out.start()
    copy_wo.wait()

    def head_step(c):
        @pl.when(is_top)
        def _():
            top_local(c).wait()
            for k in range(1, tensors):
                arrival(c, wrap(t + k, tensors)).wait_recv()

        @pl.when(jnp.logical_not(is_top))
        def _():
            for k in range(tensors):
                arrival(c, k).wait_recv()

        @pl.loop(0, heads // HEAD_TILE)
        def _(j):
            tile = pl.ds(pl.multiple_of(j * HEAD_TILE, HEAD_TILE), HEAD_TILE)
            part = lax.dot_general(
                gbuf[row(c), :], wo[tile, :], (((1,), (1,)), ((), ())),
                preferred_element_type=jnp.float32)
            hg[:, tile] = part
            dp_out[row(c), tile] = part.astype(jnp.bfloat16)

        for k in range(1, dps):
            dp_copy(c, k).start()

    def delta_step(c):
        @pl.when(c == 0)
        def _():
            copy_wi.wait()

        for k in range(1, dps):
            dp_copy(c, k).wait_recv()
        total = hg[...]
        for k in range(1, dps):
            total = total + dp_in[k - 1, row(c), :].astype(jnp.float32)
        hd[row(c), :] = (total * slope[row(c), :]).astype(jnp.bfloat16)

        for k in list(range(1, tensors)) + [0]:
            target = column(wrap(t + k, tensors))
            rs_out[row(c), target] = jnp.dot(
                hd[row(c), :], wi[:, target], preferred_element_type=jnp.float32
            ).astype(jnp.bfloat16)
            if k:
                rs_copy(c, k).start()

    def sum_step(c):
        for k in range(1, tensors):
            rs_copy(c, k).wait_recv()
        summed = rs_out[row(c), column(t)].astype(jnp.float32)
        for k in range(1, tensors):
            summed = summed + rs_in[k - 1, row(c), :].astype(jnp.float32)
        newg[row(c), :] = (
            gbuf[row(c), column(t)].astype(jnp.float32) + summed).astype(jnp.bfloat16)

        @pl.when(has_next)
        def _():
            for k in range(tensors):
                relay_copy(c, k).start()

    head_step(0)

    @pl.loop(0, chunks)
    def _(c):
        delta_step(c)
        pl.when(c + 1 < chunks)(lambda: head_step(c + 1))
        sum_step(c)

    @pl.when(jnp.logical_not(early))
    def _():
        for k in range(1, tensors):
            x_copy(k).start()

    outs = [
        pltpu.make_async_copy(gbuf, gall_o, out_sem.at[1]),
        pltpu.make_async_copy(hd, hd_o, out_sem.at[2]),
        pltpu.make_async_copy(newg, sg_o, out_sem.at[3]),
    ]
    for copy in outs:
        copy.start()

    for m in range(micro):
        for k in range(1, dps):
            pre_copy(m, k).wait_send()

    @pl.loop(0, chunks)
    def _(c):
        for k in range(1, dps):
            dp_copy(c, k).wait_send()
        for k in range(1, tensors):
            rs_copy(c, k).wait_send()

        @pl.when(is_top)
        def _():
            for k in range(1, tensors):
                top_copy(c, k).wait_send()

        @pl.when(has_next)
        def _():
            for k in range(tensors):
                relay_copy(c, k).wait_send()

    x_out.wait()
    act_out.wait()
    for copy in outs:
        copy.wait()
    for k in range(1, tensors):
        x_copy(k).wait_send()
        x_arrival(k).wait_recv()


def chain(sizes, gtop, pre, inputs, win, wout):
    sections, dps, tensors = sizes
    rows, cols = gtop.shape
    micro, block_rows, heads = pre.shape
    wide = wout.shape[1]
    chunks = rows // CHUNK
    dims = (sections, dps, tensors, chunks, CHUNK, micro, block_rows)
    bf16, f32 = jnp.bfloat16, jnp.float32
    anywhere = pl.BlockSpec(memory_space=pl.ANY)
    dma = pltpu.SemaphoreType.DMA
    return pl.pallas_call(
        functools.partial(chain_kernel, dims),
        out_shape=(
            jax.ShapeDtypeStruct((rows, wide), bf16),
            jax.ShapeDtypeStruct((rows, wide), bf16),
            jax.ShapeDtypeStruct((rows, heads), bf16),
            jax.ShapeDtypeStruct((rows, heads), bf16),
            jax.ShapeDtypeStruct((rows, cols), bf16),
        ),
        in_specs=[anywhere] * 5,
        out_specs=(anywhere,) * 5,
        scratch_shapes=[
            pltpu.VMEM((heads, wide), bf16),
            pltpu.VMEM((heads, wide), bf16),
            pltpu.VMEM((rows, wide), bf16),
            pltpu.VMEM((rows, wide), bf16),
            pltpu.VMEM((tensors - 1, rows, cols), bf16),
            pltpu.VMEM((rows, heads), bf16),
            pltpu.VMEM((dps - 1, rows, heads), bf16),
            pltpu.VMEM((rows, heads), f32),
            pltpu.VMEM((CHUNK, heads), f32),
            pltpu.VMEM((rows, heads), bf16),
            pltpu.VMEM((rows, heads), bf16),
            pltpu.VMEM((rows, heads), bf16),
            pltpu.VMEM((rows, cols), bf16),
            pltpu.VMEM((rows, cols), bf16),
            dma((2,)),
            dma((chunks, tensors - 1)),
            dma((chunks,)),
            dma((chunks, tensors)),
            dma((chunks, tensors)),
            dma((chunks, tensors - 1)),
            dma((chunks, tensors - 1)),
            dma((chunks, dps - 1)),
            dma((chunks, dps - 1)),
            dma((micro, dps - 1)),
            dma((micro, dps - 1)),
            dma((micro,)),
            dma((tensors - 1,)),
            dma((tensors - 1,)),
            dma((2,)),
            dma((4,)),
        ],
        compiler_params=pltpu.CompilerParams(
            collective_id=0, has_side_effects=True, vmem_limit_bytes=VMEM_BYTES),
        name="chain",
    )(gtop, pre, inputs, win, wout)


def kernel_fits(sizes, grad_top, pre, weight_out):
    sections, dps, tensors = sizes
    micro, tokens, cols = grad_top.shape
    heads, wide = weight_out.shape[1:]
    rows = micro * tokens
    need = 4 * heads * wide + 2 * rows * (3 * wide + (7 + dps) * heads + 2 * cols)
    return (
        dps > 1 and tensors > 1 and sections > 1
        and cols % COL_TILE == 0 and heads % HEAD_TILE == 0
        and rows % CHUNK == 0 and pre.shape[2] % 16 == 0
        and need + 4 * CHUNK * heads < VMEM_BYTES - 2**21
    )


def on_device(grad_top, inputs, pre, weight_in, weight_out):
    sizes = tuple(lax.axis_size(name) for name in ("pipe", "dp", "tensor"))
    if not kernel_fits(sizes, grad_top, pre, weight_out):
        return general_device(grad_top, inputs, pre, weight_in, weight_out)
    cols = grad_top.shape[-1]
    gall, xall, head_delta, activated, new_grad = chain(
        sizes,
        grad_top.reshape(-1, cols),
        pre[0],
        inputs[0].reshape(-1, cols),
        weight_in[0],
        weight_out[0],
    )
    contract = (((0,), (0,)), ((), ()))
    grad_out = lax.dot_general(activated, gall, contract, preferred_element_type=jnp.float32)
    grad_in = lax.dot_general(head_delta, xall, contract, preferred_element_type=jnp.float32)
    return (
        grad_in.astype(jnp.bfloat16)[None],
        grad_out.astype(jnp.bfloat16)[None],
        new_grad.reshape(grad_top.shape)[None],
    )


def solution(mesh):
    placed = (
        P(None, None, ("dp", "tensor")),
        P("pipe", None, None, ("dp", "tensor")),
        P("pipe", None, "dp", "tensor"),
        P("pipe", "tensor", "dp"),
        P("pipe", "tensor", "dp"),
    )
    return jax.shard_map(
        on_device,
        mesh=mesh,
        in_specs=placed,
        out_specs=(
            P("pipe", "tensor", "dp"),
            P("pipe", "tensor", "dp"),
            P("pipe", None, None, ("dp", "tensor")),
        ),
        check_vma=False,
    )
```
